128 devices in a mesh: row: 8 (over z, core), col: 16 (over x, y).
Axes of the slice: x: 4, y: 4, z: 4, core: 2. Of those that a mesh axis runs over, the one named last changes fastest.
Arguments:
- tokens: bfloat16 [1024, 12288], P('row', 'col'), may hold values from -6 to 6
- up_weight: bfloat16 [1024, 49152], P('row', 'col'), may hold values from -0.1875 to 0.1875
- down_weight: bfloat16 [1024, 49152], P('row', 'col'), may hold values from -0.09375 to 0.09375
- up_index: int32 [8, 384], P(None, 'col'), may hold values from 0 to 95, as said below
- down_index: int32 [8, 384], P(None, 'col'), may hold values from 0 to 95, as said below
- up_bias: float32 [49152], P('col'), may hold values from -3 to 3
- down_bias: float32 [12288], P('col'), may hold values from -3 to 3
Outputs:
- mixed: bfloat16 [1024, 12288], P('row', 'col')
The draws below stay inside these ranges and needn't reach their ends.
Inputs may be any that keep to these rules, and one draw needn't show every extreme that they name: For each block column c the 8 entries up_index[:, c] are distinct, and for each slot s the entries over any 96 consecutive block columns are distinct. For each block row r the 8 entries down_index[:, r] are distinct, and for each slot s the entries over any 96 consecutive block rows are distinct.
All inputs are finite; a program needn't handle non-finite values.
Results may differ from the reference program's by a relative error of at most 0.015.
Values may be sent and summed in bfloat16 or wider, within the bound.
A program may use at most 128 MiB of HBM per device.

```python
import jax
import jax.numpy as jnp
from jax import lax

D = 12288
FF = 49152
BLK = 128
KB = 8
TOKENS = 1024
DB = 96
FB = 384
N_COL = 16


def pattern(key, seed_tag):
    folded = jax.random.fold_in(key, seed_tag)
    first_key, second_key = jax.random.split(folded)
    relabel = jax.random.permutation(first_key, DB)
    offsets = jax.random.permutation(second_key, DB)[:KB]
    columns = jnp.arange(FB, dtype=jnp.int32)
    return relabel[(columns[None, :] + offsets[:, None]) % DB].astype(jnp.int32)


def draw_up_index(key, part):
    return pattern(key, 11)


def draw_down_index(key, part):
    return pattern(key, 23)


def level_of(stream_key, dims, cuts, smallest, largest):
    loudness, own = 1.0, jax.random.fold_in(stream_key, 6)
    for axis_at, parts in cuts:
        heights = jnp.exp(jax.random.uniform(jax.random.fold_in(own, axis_at), (parts,), jnp.float32, smallest / len(cuts), largest / len(cuts)))
        loudness = loudness * jnp.repeat(heights, dims[axis_at] // parts).reshape([-1 if axis == axis_at else 1 for axis in range(len(dims))])
    return loudness


def normal_values(own_key, shape, deviation, reach, pieces=(), held_as=jnp.bfloat16):
    values = jax.random.normal(own_key, shape, jnp.float32) * deviation
    if len(pieces) > 0:
        values = level_of(own_key, shape, pieces, -0.22, 0.18) * values
    return jnp.clip(values, min=-reach, max=reach).astype(held_as)


def setup_inputs(seed: int = 0) -> dict:
    keys = jax.random.split(jax.random.key(seed), 8)
    tokens = normal_values(keys[0], (TOKENS, D), 1.0, 6.0, ((0, 8), (1, 16)))
    up_weight = normal_values(keys[1], (KB * BLK, FF), (KB * BLK) ** -0.5, 0.1875, ((0, 8), (1, 16)))
    down_weight = normal_values(keys[2], (KB * BLK, FF), (FF * KB // D * BLK) ** -0.5, 0.09375, ((0, 8), (1, 16)))
    up_index = draw_up_index(jax.random.fold_in(keys[7], 71), 0)
    down_index = draw_down_index(jax.random.fold_in(keys[7], 71), 0)
    up_bias = normal_values(keys[5], (FF,), 0.5, 3.0, ((0, 16),), jnp.float32)
    down_bias = normal_values(keys[6], (D,), 0.5, 3.0, ((0, 16),), jnp.float32)
    return dict(tokens=tokens, up_weight=up_weight, down_weight=down_weight, up_index=up_index, down_index=down_index, up_bias=up_bias, down_bias=down_bias)


def reference(tokens, up_weight, down_weight, up_index, down_index, up_bias, down_bias):
    features = tokens.reshape(TOKENS, DB, BLK).astype(jnp.float32)
    up_grid = up_weight.reshape(KB, BLK, FB, BLK).astype(jnp.float32)
    down_grid = down_weight.reshape(KB, BLK, FB, BLK).astype(jnp.float32)
    bias_grid = up_bias.astype(jnp.float32).reshape(FB, BLK)
    per_shard = FB // N_COL

    def shard(running, shard_index):
        offset_col = shard_index * per_shard
        preact = jnp.zeros((TOKENS, per_shard, BLK), jnp.float32)
        for slot_index in range(KB):
            columns = lax.dynamic_slice_in_dim(up_index[slot_index], offset_col, per_shard, 0).astype(jnp.int32)
            selected = jnp.take(features, columns, axis=1)
            panels = lax.dynamic_slice_in_dim(up_grid[slot_index], offset_col, per_shard, 1)
            preact = preact + jnp.einsum("tck,kcn->tcn", selected, panels)
        preact = preact + lax.dynamic_slice_in_dim(bias_grid, offset_col, per_shard, 0)[None]
        hidden = jax.nn.gelu(preact, approximate=True).astype(jnp.bfloat16)
        hidden = lax.optimization_barrier(hidden).astype(jnp.float32)
        partial_value = jnp.zeros((TOKENS, DB, BLK), jnp.float32)
        for slot_index in range(KB):
            panels = lax.dynamic_slice_in_dim(down_grid[slot_index], offset_col, per_shard, 1)
            product = jnp.einsum("trk,nrk->trn", hidden, panels)
            targets = lax.dynamic_slice_in_dim(down_index[slot_index], offset_col, per_shard, 0).astype(jnp.int32)
            partial_value = partial_value.at[:, targets].add(product)
        partial_value = partial_value.astype(jnp.bfloat16)
        partial_value = lax.optimization_barrier(partial_value).astype(jnp.float32)
        return running + partial_value, None

    running, unused = lax.scan(shard, jnp.zeros((TOKENS, DB, BLK), jnp.float32), jnp.arange(N_COL, dtype=jnp.int32))
    result = running.reshape(TOKENS, D) + down_bias.astype(jnp.float32)[None]
    return result.astype(jnp.bfloat16)
```

```python
import jax
import jax.numpy as jnp
from jax import lax
from jax.experimental import pallas as pl
from jax.experimental.pallas import tpu as pltpu
from jax.sharding import PartitionSpec as P

BLK = 128
KB = 8
N = 4
DB = 96
CB = 24
OB = 6
HB = 3
TOK = 128
Q = 4
CH = BLK // Q
HH = CH // 2
NSEM = 220
MESH = pl.DeviceIdType.MESH
F32 = jnp.float32
BF16 = jnp.bfloat16


def kernel(up_idx, inv, tok, up, dn, ub, db, out,
           feat, wu, wd, acc, ht, prod, outp, r1, o2, r2, res, ssem, rsem, lsem):
    row = lax.axis_index("row")
    col = lax.axis_index("col")
    z, k = row // 2, row % 2
    x, y = col // N, col % N
    slot = lambda dz: ((z + dz + N) % N) * 2 + k
    cidx = lambda dx, dy: ((x + dx + N) % N) * N + (y + dy + N) % N
    zp, zm, pr = (slot(1), col), (slot(-1), col), (z * 2 + 1 - k, col)
    xp, xm = (row, cidx(1, 0)), (row, cidx(-1, 0))
    yp, ym = (row, cidx(0, 1)), (row, cidx(0, -1))

    local = []

    def lcopy(src, dst):
        c = pltpu.make_async_copy(src, dst, lsem.at[len(local)])
        c.start()
        local.append(c)
        return c

    tok_in = [lcopy(tok.at[:, pl.ds(j * BLK, BLK)], feat.at[col * OB + j]) for j in range(OB)]
    up_in = lcopy(up, wu.at[row])
    dn_in = lcopy(dn, wd.at[row])

    barrier = pltpu.get_barrier_semaphore()
    for dev in (zp, zm, pr, xp, xm, yp, ym):
        pl.semaphore_signal(barrier, inc=1, device_id=dev, device_id_type=MESH)
    pl.semaphore_wait(barrier, 7)

    sent = []

    def rcopy(src, dst, dev):
        i = len(sent)
        c = pltpu.make_async_remote_copy(
            src_ref=src, dst_ref=dst, send_sem=ssem.at[i], recv_sem=rsem.at[i],
            device_id=dev, device_id_type=MESH)
        c.start()
        sent.append(c)
        return c

    def same(ref, dev):
        return rcopy(ref, ref, dev)

    half = BLK // 2
    ur = lambda h: pl.ds(h * half, half)
    u_p = [rcopy(up.at[ur(h)], wu.at[row, ur(h)], zp) for h in (0, 1)]
    u_m = [rcopy(up.at[ur(h)], wu.at[row, ur(h)], zm) for h in (1, 0)]
    u_c = rcopy(up, wu.at[row], pr)

    for c in tok_in:
        c.wait()

    def chunk(h, da, db_):
        dx, dy = (da, db_) if h == 0 else (db_, da)
        return pl.ds(cidx(dx, dy) * OB + h * HB, HB)

    ax1 = ((xp, xm), (yp, ym))
    ax2 = ((yp, ym), (xp, xm))
    t_own = [[same(feat.at[chunk(h, 0, 0)], d) for d in ax1[h]] for h in (0, 1)]
    t2 = [[[], []], [[], []]]

    def spread(h, da):
        for i, d in enumerate(ax2[h]):
            t2[h][i].append(same(feat.at[chunk(h, da, 0)], d))

    for h in (0, 1):
        spread(h, 0)

    dr = lambda q: pl.ds(q * CH, CH)
    d_own = {}

    def d_issue(q):
        if q < Q:
            d_own[q] = [rcopy(dn.at[dr(q)], wd.at[row, dr(q)], d) for d in (zp, zm)]

    d_issue(0)
    d_c = rcopy(dn, wd.at[row], pr)

    tr = lambda i: pl.ds(i * (TOK // 2), TOK // 2)
    t_fwd = [[], []]
    for h in (0, 1):
        for i in (0, 1):
            t_own[h][i].wait_recv()
            da = -1 if i == 0 else 1
            t_fwd[h].append(same(feat.at[chunk(h, da, 0), tr(i)], ax1[h][i]))
        spread(h, -1)
        spread(h, 1)
    for h in (0, 1):
        for c in t_fwd[h]:
            c.wait_recv()
        spread(h, 2)

    u_p[0].wait_recv()
    u_m[0].wait_recv()
    u_f = [same(wu.at[slot(-1), ur(0)], zp), same(wu.at[slot(1), ur(1)], zm)]
    d_issue(1)

    t2_fwd = [[], []]
    for n, da in enumerate((0, -1, 1, 2)):
        for h in (0, 1):
            for i in (0, 1):
                t2[h][i][n].wait_recv()
                t2_fwd[h].append(
                    same(feat.at[chunk(h, da, -1 if i == 0 else 1), tr(i)], ax2[h][i]))

    prod[:, CB] = jnp.zeros((KB, CH, TOK), F32)
    u_p[1].wait_recv()
    u_m[1].wait_recv()
    u_n = [same(wu.at[slot(-1)], pr), same(wu.at[slot(1)], pr)]
    for h in (0, 1):
        for c in t2_fwd[h]:
            c.wait_recv()
    up_in.wait()
    u_c.wait_recv()
    for c in u_n:
        c.wait_recv()

    zpair = lambda dz: (z + dz + N) % N

    def up_dot(p, c):
        xs = jnp.concatenate([feat[up_idx[2 * p, c]], feat[up_idx[2 * p + 1, c]]], axis=1)
        w = wu[pl.ds(2 * p, 2), :, pl.ds(pl.multiple_of(c * BLK, BLK), BLK)]
        return jnp.dot(xs, w.reshape(2 * BLK, BLK), preferred_element_type=F32)

    def up_first(c, carry):
        acc[c] = up_dot(zpair(0), c) + up_dot(zpair(-1), c) + up_dot(zpair(1), c)
        return carry

    lax.fori_loop(0, CB, up_first, 0)

    d_fwd, d_n, d_far = {}, {}, {}
    hr = lambda q, i: pl.ds(q * CH + i * HH, HH)

    def d_near(q):
        for c in d_own[q]:
            c.wait_recv()
        d_fwd[q] = [same(wd.at[slot(-1), hr(q, 0)], zp), same(wd.at[slot(1), hr(q, 1)], zm)]
        d_issue(q + 2)
        d_n[q] = [same(wd.at[slot(-1), dr(q)], pr), same(wd.at[slot(1), dr(q)], pr)]

    d_near(0)
    for c in u_f:
        c.wait_recv()
    u_far = same(wu.at[slot(2)], pr)
    u_far.wait_recv()

    def up_last(c, carry):
        cols = pl.ds(pl.multiple_of(c * BLK, BLK), BLK)
        v = acc[c] + up_dot(zpair(2), c) + ub[:, cols]
        g = 0.5 * v * (1.0 + jnp.tanh(0.7978845608028654 * (v + 0.044715 * (v * v * v))))
        ht[c] = g.T.astype(BF16)
        return carry

    lax.fori_loop(0, CB, up_last, 0)

    def down_dot(q, p, r):
        w = wd[pl.ds(2 * p, 2), dr(q), pl.ds(pl.multiple_of(r * BLK, BLK), BLK)]
        o = jnp.dot(w.reshape(2 * CH, BLK), ht[r], preferred_element_type=F32)
        prod[pl.ds(2 * p, 2), r] = o.reshape(2, CH, TOK)

    def down_near(q):
        def body(r, carry):
            for dz in (0, -1, 1):
                down_dot(q, zpair(dz), r)
            return carry
        lax.fori_loop(0, CB, body, 0)

    def down_far(q):
        def body(r, carry):
            down_dot(q, zpair(2), r)
            return carry
        lax.fori_loop(0, CB, body, 0)

    def place(q):
        def body(g, carry):
            for j in range(OB):
                d = g * OB + j
                v = prod[0, inv[0, d]]
                for s in range(1, KB):
                    v = v + prod[s, inv[s, d]]
                v = v.astype(BF16)
                for i in (0, 1):
                    outp[q, i, g // N, g % N, j] = v[i * HH:(i + 1) * HH]
            return carry
        lax.fori_loop(0, N * N, body, 0)

    rs1, rs2 = {}, {}
    rx1 = ((yp, ym), (xp, xm))
    rx2 = ((xp, xm), (yp, ym))
    apos = lambda h, da: ((y if h == 0 else x) + da + N) % N
    bpos = lambda h, da: ((x if h == 0 else y) + da + N) % N

    def src1(q, h, da, i):
        if h == 0:
            return outp.at[q, i, :, apos(h, da), pl.ds(0, HB)]
        return outp.at[q, i, apos(h, da), :, pl.ds(HB, HB)]

    def src2(q, h, da, i):
        return o2.at[q, h, i, bpos(h, da)]

    def open_ring(q, h, src, buf, dirs, book):
        p, m = dirs[h]
        book[q, h] = {
            0: rcopy(src(q, h, 2, 0), buf.at[q, h, 0], p),
            1: rcopy(src(q, h, 2, 1), buf.at[q, h, 1], m),
            3: rcopy(src(q, h, 1, 1), buf.at[q, h, 3], p),
            4: rcopy(src(q, h, -1, 0), buf.at[q, h, 4], m),
        }

    def turn_ring(q, h, src, buf, dirs, book):
        p, m = dirs[h]
        b = book[q, h]
        for got, da, i, to, dev in ((0, 1, 0, 2, p), (1, -1, 1, 5, m)):
            b[got].wait_recv()
            s = src(q, h, da, i)
            s[...] = (s[...].astype(F32) + buf[q, h, got].astype(F32)).astype(BF16)
            b[to] = rcopy(s, buf.at[q, h, to], dev)

    def close_ring(q, h, src, buf, book, i):
        a, b = (2, 4) if i == 0 else (3, 5)
        book[q, h][a].wait_recv()
        book[q, h][b].wait_recv()
        return (src(q, h, 0, i)[...].astype(F32) + buf[q, h, a].astype(F32)
                + buf[q, h, b].astype(F32))

    def rs_a(q):
        for h in (0, 1):
            open_ring(q, h, src1, r1, rx1, rs1)

    def rs_b(q):
        for h in (0, 1):
            turn_ring(q, h, src1, r1, rx1, rs1)

    def rs_c(q):
        for h in (0, 1):
            for i in (0, 1):
                o2[q, h, i] = close_ring(q, h, src1, r1, rs1, i).astype(BF16)
            open_ring(q, h, src2, r2, rx2, rs2)

    def rs_d(q):
        for h in (0, 1):
            turn_ring(q, h, src2, r2, rx2, rs2)

    def rs_e(q):
        for h in (0, 1):
            for i in (0, 1):
                res[pl.ds(h * HB, HB), hr(q, i)] = close_ring(q, h, src2, r2, rs2, i)

    dn_in.wait()
    d_c.wait_recv()
    for q in range(Q):
        if q > 0:
            d_near(q)
        for c in d_n[q]:
            c.wait_recv()
        down_near(q)
        if q > 0:
            rs_b(q - 1)
        for c in d_fwd[q]:
            c.wait_recv()
        d_far[q] = same(wd.at[slot(2), dr(q)], pr)
        if q > 0:
            rs_c(q - 1)
        d_far[q].wait_recv()
        down_far(q)
        place(q)
        rs_a(q)
        if q > 0:
            rs_d(q - 1)
            rs_e(q - 1)
    rs_b(Q - 1)
    rs_c(Q - 1)
    rs_d(Q - 1)
    rs_e(Q - 1)

    for j in range(OB):
        cols = pl.ds(j * BLK, BLK)
        out[:, cols] = (res[j].T + db[:, cols]).astype(BF16)
    for c in sent:
        c.wait_send()


def per_device(tokens, up_weight, down_weight, up_index, down_index, up_bias, down_bias):
    rows = jnp.arange(CB, dtype=jnp.int32)
    blocks = jnp.arange(DB, dtype=jnp.int32)
    hit = down_index[:, None, :] == blocks[None, :, None]
    inv = jnp.min(jnp.where(hit, rows[None, None, :], CB), axis=2)
    smem = pl.BlockSpec(memory_space=pltpu.SMEM)
    vmem = pl.BlockSpec(memory_space=pltpu.VMEM)
    hbm = pl.BlockSpec(memory_space=pl.ANY)
    return pl.pallas_call(
        kernel,
        out_shape=jax.ShapeDtypeStruct(tokens.shape, BF16),
        in_specs=[smem, smem, hbm, hbm, hbm, vmem, vmem],
        out_specs=vmem,
        scratch_shapes=[
            pltpu.VMEM((DB, TOK, BLK), BF16),
            pltpu.VMEM((KB, BLK, CB * BLK), BF16),
            pltpu.VMEM((KB, BLK, CB * BLK), BF16),
            pltpu.VMEM((CB, TOK, BLK), F32),
            pltpu.VMEM((CB, BLK, TOK), BF16),
            pltpu.VMEM((KB, CB + 1, CH, TOK), F32),
            pltpu.VMEM((Q, 2, N, N, OB, HH, TOK), BF16),
            pltpu.VMEM((Q, 2, 6, N, HB, HH, TOK), BF16),
            pltpu.VMEM((Q, 2, 2, N, HB, HH, TOK), BF16),
            pltpu.VMEM((Q, 2, 6, HB, HH, TOK), BF16),
            pltpu.VMEM((OB, BLK, TOK), F32),
            pltpu.SemaphoreType.DMA((NSEM,)),
            pltpu.SemaphoreType.DMA((NSEM,)),
            pltpu.SemaphoreType.DMA((8,)),
        ],
        compiler_params=pltpu.CompilerParams(
            collective_id=0, has_side_effects=True, vmem_limit_bytes=60 * 2**20),
    )(up_index, inv, tokens, up_weight, down_weight,
      up_bias.reshape(1, -1), down_bias.reshape(1, -1))


def solution(mesh):
    placed = (
        P("row", "col"),
        P("row", "col"),
        P("row", "col"),
        P(None, "col"),
        P(None, "col"),
        P("col"),
        P("col"),
    )
    return jax.shard_map(
        per_device, mesh=mesh, in_specs=placed, out_specs=P("row", "col"), check_vma=False
    )
```

```python
import jax
import jax.numpy as jnp
from jax import lax
from jax.experimental import pallas as pl
from jax.experimental.pallas import tpu as pltpu
from jax.sharding import PartitionSpec as P

BLK = 128
KB = 8
N = 4
DB = 96
CB = 24
OB = 6
HB = 3
TOK = 128
SIZES = (32, 32, 32, 16, 16)
STARTS = tuple(sum(SIZES[:q]) for q in range(len(SIZES)))
Q = len(SIZES)
CH = max(SIZES)
NSEM = 180
UP_UNROLL = 4
DN_UNROLL = 8
MESH = pl.DeviceIdType.MESH
F32 = jnp.float32
BF16 = jnp.bfloat16


def kernel(up_idx, dn_idx, tok, up, dn, ub, out,
           feat, wu, wd, acc, ht, prod, psum, outp, r1, o2, r2, res, inv_v, inv,
           ssem, rsem, lsem):
    row = lax.axis_index("row")
    col = lax.axis_index("col")
    z, k = row // 2, row % 2
    x, y = col // N, col % N
    slot = lambda dz: ((z + dz + N) % N) * 2 + k
    zpair = lambda dz: (z + dz + N) % N
    cidx = lambda dx, dy: ((x + dx + N) % N) * N + (y + dy + N) % N
    zp, zm, pr = (slot(1), col), (slot(-1), col), (z * 2 + 1 - k, col)
    xd = {d: (row, cidx(d, 0)) for d in (1, -1, 2)}
    yd = {d: (row, cidx(0, d)) for d in (1, -1, 2)}
    RING = (1, -1, 2)

    local = []

    def lcopy(src, dst):
        c = pltpu.make_async_copy(src, dst, lsem.at[len(local)])
        c.start()
        local.append(c)
        return c

    tok_in = [lcopy(tok.at[:, pl.ds(j * BLK, BLK)], feat.at[col * OB + j]) for j in range(OB)]
    up_in = lcopy(up, wu.at[row])
    dn_in = lcopy(dn, wd.at[row])

    barrier = pltpu.get_barrier_semaphore()
    peers = [zp, zm, pr] + list(xd.values()) + list(yd.values())
    for dev in peers:
        pl.semaphore_signal(barrier, inc=1, device_id=dev, device_id_type=MESH)

    lanes = lax.broadcasted_iota(jnp.int32, (KB, BLK), 1)
    where = jnp.full((KB, BLK), CB, jnp.int32)
    for r in range(CB):
        where = jnp.where(dn_idx[:, r:r + 1] == lanes, r, where)
    inv_v[...] = where
    prod[:, CB] = jnp.zeros((KB, CH, TOK), F32)

    pl.semaphore_wait(barrier, len(peers))

    sent = []

    def rcopy(src, dst, dev):
        i = len(sent)
        c = pltpu.make_async_remote_copy(
            src_ref=src, dst_ref=dst, send_sem=ssem.at[i], recv_sem=rsem.at[i],
            device_id=dev, device_id_type=MESH)
        c.start()
        sent.append(c)
        return c

    def same(ref, dev):
        return rcopy(ref, ref, dev)

    half = BLK // 2
    ur = lambda h: pl.ds(h * half, half)
    u_p = [rcopy(up.at[ur(h)], wu.at[row, ur(h)], zp) for h in (0, 1)]
    u_m = [rcopy(up.at[ur(h)], wu.at[row, ur(h)], zm) for h in (1, 0)]
    u_c = rcopy(up, wu.at[row], pr)

    for c in tok_in:
        c.wait()

    def chunk(h, da):
        dx, dy = (da, 0) if h == 0 else (0, da)
        return pl.ds(cidx(dx, dy) * OB + h * HB, HB)

    ring1, ring2 = (xd, yd), (yd, xd)
    t1 = [[same(feat.at[chunk(h, 0)], ring1[h][d]) for d in RING] for h in (0, 1)]
    t2 = [[], []]

    def spread(h, da):
        t2[h] += [same(feat.at[chunk(h, da)], ring2[h][d]) for d in RING]

    for h in (0, 1):
        spread(h, 0)
    for n, d in enumerate(RING):
        for h in (0, 1):
            t1[h][n].wait_recv()
            spread(h, -d)

    u_p[0].wait_recv()
    u_m[0].wait_recv()
    u_f = [same(wu.at[slot(-1), ur(0)], zp), same(wu.at[slot(1), ur(1)], zm)]

    dr = lambda q: pl.ds(STARTS[q], SIZES[q])
    d_own, d_fwd, d_n, d_far = {}, {}, {}, {}

    def d_issue(q):
        if q < Q:
            d_own[q] = [rcopy(dn.at[dr(q)], wd.at[row, dr(q)], d) for d in (zp, zm)]

    hc = lambda i: pl.ds(i * (CB * BLK // 2), CB * BLK // 2)

    def d_near(q):
        if q < Q:
            for c in d_own[q]:
                c.wait_recv()
            d_fwd[q] = [same(wd.at[slot(-1), dr(q), hc(0)], zp),
                        same(wd.at[slot(1), dr(q), hc(1)], zm)]
            d_issue(q + 2)
            d_n[q] = [same(wd.at[slot(-1), dr(q)], pr), same(wd.at[slot(1), dr(q)], pr)]

    d_issue(0)
    d_issue(1)
    d_c = rcopy(dn, wd.at[row], pr)

    inv_in = lcopy(inv_v, inv)
    u_p[1].wait_recv()
    u_m[1].wait_recv()
    u_n = [same(wu.at[slot(-1)], pr), same(wu.at[slot(1)], pr)]
    for h in (0, 1):
        for c in t2[h]:
            c.wait_recv()
    up_in.wait()
    u_c.wait_recv()
    for c in u_n:
        c.wait_recv()

    def cols(c):
        return pl.ds(pl.multiple_of(c * BLK, BLK), BLK)

    def up_dot(p, c):
        xs = jnp.concatenate([feat[up_idx[2 * p, c]], feat[up_idx[2 * p + 1, c]]], axis=1)
        w = wu[pl.ds(2 * p, 2), :, cols(c)]
        return jnp.dot(xs, w.reshape(2 * BLK, BLK), preferred_element_type=F32)

    def up_first(c, carry):
        acc[c] = up_dot(zpair(0), c) + up_dot(zpair(-1), c) + up_dot(zpair(1), c)
        return carry

    lax.fori_loop(0, CB, up_first, 0, unroll=UP_UNROLL)

    for c in u_f:
        c.wait_recv()
    u_far = same(wu.at[slot(2)], pr)
    u_far.wait_recv()

    def up_last(c, carry):
        v = acc[c] + up_dot(zpair(2), c) + ub[:, cols(c)]
        g = 0.5 * v * (1.0 + jnp.tanh(0.7978845608028654 * (v + 0.044715 * (v * v * v))))
        ht[c] = g.T.astype(BF16)
        return carry

    lax.fori_loop(0, CB, up_last, 0, unroll=UP_UNROLL)

    def down_dots(q, dzs):
        n = SIZES[q]

        def body(r, carry):
            w = jnp.concatenate(
                [wd[pl.ds(2 * zpair(dz), 2), dr(q), cols(r)].reshape(2 * n, BLK) for dz in dzs],
                axis=0)
            o = jnp.dot(w, ht[r], preferred_element_type=F32)
            for i, dz in enumerate(dzs):
                prod[pl.ds(2 * zpair(dz), 2), r, pl.ds(0, n)] = (
                    o[2 * n * i:2 * n * (i + 1)].reshape(2, n, TOK))
            return carry

        lax.fori_loop(0, CB, body, 0, unroll=DN_UNROLL)

    near, far = (0, -1, 1), (2,)

    def placed(q, d, dzs):
        terms = []
        for dz in dzs:
            for i in (0, 1):
                s = 2 * zpair(dz) + i
                terms.append(prod[s, inv[s, d], pl.ds(0, SIZES[q])])
        while len(terms) > 1:
            terms = [a + b for a, b in zip(terms[::2], terms[1::2])] + (
                [terms[-1]] if len(terms) % 2 else [])
        return terms[0]

    def place_near(q):
        def body(g, carry):
            for j in range(OB):
                d = g * OB + j
                psum[d, pl.ds(0, SIZES[q])] = placed(q, d, near)
            return carry
        lax.fori_loop(0, N * N, body, 0)

    def place_far(q):
        def body(g, carry):
            for j in range(OB):
                d = g * OB + j
                v = psum[d, pl.ds(0, SIZES[q])] + placed(q, d, far)
                outp[g // N, g % N, j, dr(q)] = v.astype(BF16)
            return carry
        lax.fori_loop(0, N * N, body, 0)

    rs1, rs2 = {}, {}

    def src1(q, h, da):
        if h == 0:
            return outp.at[:, (y + da + N) % N, pl.ds(0, HB), dr(q)]
        return outp.at[(x + da + N) % N, :, pl.ds(HB, HB), dr(q)]

    def src2(q, h, db):
        return o2.at[h, ((x if h == 0 else y) + db + N) % N, :, dr(q)]

    def rs_a(q):
        for n, d in enumerate(RING):
            for h in (0, 1):
                rs1[q, h, n] = rcopy(src1(q, h, d), r1.at[h, n, :, :, dr(q)], ring2[h][d])

    def rs_b(q):
        for h in (0, 1):
            total = src1(q, h, 0)[...].astype(F32)
            for n in range(3):
                rs1[q, h, n].wait_recv()
                total = total + r1[h, n, :, :, dr(q)].astype(F32)
            o2[h, :, :, dr(q)] = total.astype(BF16)
            for n, d in enumerate(RING):
                rs2[q, h, n] = rcopy(src2(q, h, d), r2.at[h, n, :, dr(q)], ring1[h][d])

    def rs_c(q):
        for h in (0, 1):
            total = src2(q, h, 0)[...].astype(F32)
            for n in range(3):
                rs2[q, h, n].wait_recv()
                total = total + r2[h, n, :, dr(q)].astype(F32)
            res[pl.ds(h * HB, HB), dr(q)] = total

    inv_in.wait()
    dn_in.wait()
    d_c.wait_recv()
    d_near(0)
    for q in range(Q):
        for c in d_n[q]:
            c.wait_recv()
        down_dots(q, near)
        place_near(q)
        d_near(q + 1)
        if q > 0:
            rs_b(q - 1)
        for c in d_fwd[q]:
            c.wait_recv()
        d_far[q] = same(wd.at[slot(2), dr(q)], pr)
        d_far[q].wait_recv()
        down_dots(q, far)
        place_far(q)
        rs_a(q)
        if q > 0:
            rs_c(q - 1)
    rs_b(Q - 1)
    rs_c(Q - 1)

    for j in range(OB):
        out[:, pl.ds(j * BLK, BLK)] = res[j].T
    for c in sent:
        c.wait_send()


def per_device(tokens, up_weight, down_weight, up_index, down_index, up_bias, down_bias):
    smem = pl.BlockSpec(memory_space=pltpu.SMEM)
    vmem = pl.BlockSpec(memory_space=pltpu.VMEM)
    hbm = pl.BlockSpec(memory_space=pl.ANY)
    total = pl.pallas_call(
        kernel,
        out_shape=jax.ShapeDtypeStruct(tokens.shape, F32),
        in_specs=[smem, vmem, hbm, hbm, hbm, vmem],
        out_specs=vmem,
        scratch_shapes=[
            pltpu.VMEM((DB, TOK, BLK), BF16),
            pltpu.VMEM((KB, BLK, CB * BLK), BF16),
            pltpu.VMEM((KB, BLK, CB * BLK), BF16),
            pltpu.VMEM((CB, TOK, BLK), F32),
            pltpu.VMEM((CB, BLK, TOK), BF16),
            pltpu.VMEM((KB, CB + 1, CH, TOK), F32),
            pltpu.VMEM((DB, CH, TOK), F32),
            pltpu.VMEM((N, N, OB, BLK, TOK), BF16),
            pltpu.VMEM((2, 3, N, HB, BLK, TOK), BF16),
            pltpu.VMEM((2, N, HB, BLK, TOK), BF16),
            pltpu.VMEM((2, 3, HB, BLK, TOK), BF16),
            pltpu.VMEM((OB, BLK, TOK), F32),
            pltpu.VMEM((KB, BLK), jnp.int32),
            pltpu.SMEM((KB, BLK), jnp.int32),
            pltpu.SemaphoreType.DMA((NSEM,)),
            pltpu.SemaphoreType.DMA((NSEM,)),
            pltpu.SemaphoreType.DMA((9,)),
        ],
        compiler_params=pltpu.CompilerParams(
            collective_id=0, has_side_effects=True, vmem_limit_bytes=48 * 2**20),
    )(up_index, down_index, tokens, up_weight, down_weight, up_bias.reshape(1, -1))
    return (total + down_bias[None]).astype(BF16)


def solution(mesh):
    placed = (
        P("row", "col"),
        P("row", "col"),
        P("row", "col"),
        P(None, "col"),
        P(None, "col"),
        P("col"),
        P("col"),
    )
    return jax.shard_map(
        per_device, mesh=mesh, in_specs=placed, out_specs=P("row", "col"), check_vma=False
    )
```

```python
import jax
import jax.numpy as jnp
from jax import lax
from jax.experimental import pallas as pl
from jax.experimental.pallas import tpu as pltpu
from jax.sharding import PartitionSpec as P

BLK = 128
KB = 8
N = 4
DB = 96
CB = 24
OB = 6
HB = 3
TOK = 128
SIZES = (32, 32, 32, 16, 16)
STARTS = tuple(sum(SIZES[:q]) for q in range(len(SIZES)))
Q = len(SIZES)
CH = max(SIZES)
NSEM = 180
UP_UNROLL = 4
DN_UNROLL = 8
MESH = pl.DeviceIdType.MESH
F32 = jnp.float32
BF16 = jnp.bfloat16


def kernel(up_idx, dn_idx, tok, up, dn, ub, out,
           feat, wu, wd, acc, ht, prod, psum, outp, r1, o2, r2, res, inv_v, inv,
           ssem, rsem, lsem):
    row = lax.axis_index("row")
    col = lax.axis_index("col")
    z, k = row // 2, row % 2
    x, y = col // N, col % N
    slot = lambda dz: ((z + dz + N) % N) * 2 + k
    zpair = lambda dz: (z + dz + N) % N
    cidx = lambda dx, dy: ((x + dx + N) % N) * N + (y + dy + N) % N
    zp, zm, pr = (slot(1), col), (slot(-1), col), (z * 2 + 1 - k, col)
    xd = {d: (row, cidx(d, 0)) for d in (1, -1, 2)}
    yd = {d: (row, cidx(0, d)) for d in (1, -1, 2)}
    RING = (1, -1, 2)

    local = []

    def lcopy(src, dst):
        c = pltpu.make_async_copy(src, dst, lsem.at[len(local)])
        c.start()
        local.append(c)
        return c

    tok_in = [lcopy(tok.at[:, pl.ds(j * BLK, BLK)], feat.at[col * OB + j]) for j in range(OB)]
    up_in = lcopy(up, wu.at[row])
    dn_in = lcopy(dn, wd.at[row])

    barrier = pltpu.get_barrier_semaphore()
    peers = [zp, zm, pr] + list(xd.values()) + list(yd.values())
    for dev in peers:
        pl.semaphore_signal(barrier, inc=1, device_id=dev, device_id_type=MESH)

    lanes = lax.broadcasted_iota(jnp.int32, (KB, BLK), 1)
    where = jnp.full((KB, BLK), CB, jnp.int32)
    for r in range(CB):
        where = jnp.where(dn_idx[:, r:r + 1] == lanes, r, where)
    inv_v[...] = where
    prod[:, CB] = jnp.zeros((KB, CH, TOK), F32)

    pl.semaphore_wait(barrier, len(peers))

    sent = []

    def rcopy(src, dst, dev):
        i = len(sent)
        c = pltpu.make_async_remote_copy(
            src_ref=src, dst_ref=dst, send_sem=ssem.at[i], recv_sem=rsem.at[i],
            device_id=dev, device_id_type=MESH)
        c.start()
        sent.append(c)
        return c

    def same(ref, dev):
        return rcopy(ref, ref, dev)

    half = BLK // 2
    ur = lambda h: pl.ds(h * half, half)
    u_p = [rcopy(up.at[ur(h)], wu.at[row, ur(h)], zp) for h in (0, 1)]
    u_m = [rcopy(up.at[ur(h)], wu.at[row, ur(h)], zm) for h in (1, 0)]
    u_c = rcopy(up, wu.at[row], pr)

    for c in tok_in:
        c.wait()

    def chunk(h, da):
        dx, dy = (da, 0) if h == 0 else (0, da)
        return pl.ds(cidx(dx, dy) * OB + h * HB, HB)

    ring1, ring2 = (xd, yd), (yd, xd)
    t1 = [[same(feat.at[chunk(h, 0)], ring1[h][d]) for d in RING] for h in (0, 1)]
    t2 = [[], []]

    def spread(h, da):
        t2[h] += [same(feat.at[chunk(h, da)], ring2[h][d]) for d in RING]

    for h in (0, 1):
        spread(h, 0)
    for n, d in enumerate(RING):
        for h in (0, 1):
            t1[h][n].wait_recv()
            spread(h, -d)

    u_p[0].wait_recv()
    u_m[0].wait_recv()
    u_f = [same(wu.at[slot(-1), ur(0)], zp), same(wu.at[slot(1), ur(1)], zm)]

    dr = lambda q: pl.ds(STARTS[q], SIZES[q])
    d_own, d_fwd, d_n, d_far = {}, {}, {}, {}

    def d_issue(q):
        if q < Q:
            d_own[q] = [rcopy(dn.at[dr(q)], wd.at[row, dr(q)], d) for d in (zp, zm)]

    hc = lambda i: pl.ds(i * (CB * BLK // 2), CB * BLK // 2)

    def d_near(q):
        if q < Q:
            for c in d_own[q]:
                c.wait_recv()
            d_fwd[q] = [same(wd.at[slot(-1), dr(q), hc(0)], zp),
                        same(wd.at[slot(1), dr(q), hc(1)], zm)]
            d_issue(q + 2)
            d_n[q] = [same(wd.at[slot(-1), dr(q)], pr), same(wd.at[slot(1), dr(q)], pr)]

    d_issue(0)
    d_issue(1)
    d_c = rcopy(dn, wd.at[row], pr)

    inv_in = lcopy(inv_v, inv)
    u_p[1].wait_recv()
    u_m[1].wait_recv()
    u_n = [same(wu.at[slot(-1)], pr), same(wu.at[slot(1)], pr)]
    for h in (0, 1):
        for c in t2[h]:
            c.wait_recv()
    up_in.wait()
    u_c.wait_recv()
    for c in u_n:
        c.wait_recv()

    def cols(c):
        return pl.ds(pl.multiple_of(c * BLK, BLK), BLK)

    def up_dot(p, c):
        xs = jnp.concatenate([feat[up_idx[2 * p, c]], feat[up_idx[2 * p + 1, c]]], axis=1)
        w = wu[pl.ds(2 * p, 2), :, cols(c)]
        return jnp.dot(xs, w.reshape(2 * BLK, BLK), preferred_element_type=F32)

    def up_first(c, carry):
        acc[c] = up_dot(zpair(0), c) + up_dot(zpair(-1), c) + up_dot(zpair(1), c)
        return carry

    lax.fori_loop(0, CB, up_first, 0, unroll=UP_UNROLL)

    for c in u_f:
        c.wait_recv()
    u_far = same(wu.at[slot(2)], pr)
    u_far.wait_recv()

    def up_last(c, carry):
        v = acc[c] + up_dot(zpair(2), c) + ub[:, cols(c)]
        g = 0.5 * v * (1.0 + jnp.tanh(0.7978845608028654 * (v + 0.044715 * (v * v * v))))
        ht[c] = g.T.astype(BF16)
        return carry

    lax.fori_loop(0, CB // 2, up_last, 0, unroll=UP_UNROLL)
    d_near(0)
    lax.fori_loop(CB // 2, CB, up_last, 0, unroll=UP_UNROLL)

    def down_dots(q, dzs):
        n = SIZES[q]

        def body(r, carry):
            w = jnp.concatenate(
                [wd[pl.ds(2 * zpair(dz), 2), dr(q), cols(r)].reshape(2 * n, BLK) for dz in dzs],
                axis=0)
            o = jnp.dot(w, ht[r], preferred_element_type=F32)
            for i, dz in enumerate(dzs):
                prod[pl.ds(2 * zpair(dz), 2), r, pl.ds(0, n)] = (
                    o[2 * n * i:2 * n * (i + 1)].reshape(2, n, TOK))
            return carry

        lax.fori_loop(0, CB, body, 0, unroll=DN_UNROLL)

    near, far = (0, -1, 1), (2,)

    def placed(q, d, dzs):
        terms = []
        for dz in dzs:
            for i in (0, 1):
                s = 2 * zpair(dz) + i
                terms.append(prod[s, inv[s, d], pl.ds(0, SIZES[q])])
        while len(terms) > 1:
            terms = [a + b for a, b in zip(terms[::2], terms[1::2])] + (
                [terms[-1]] if len(terms) % 2 else [])
        return terms[0]

    def place_near(q):
        def body(g, carry):
            for j in range(OB):
                d = g * OB + j
                psum[d, pl.ds(0, SIZES[q])] = placed(q, d, near)
            return carry
        lax.fori_loop(0, N * N, body, 0)

    def place_far(q):
        def body(g, carry):
            for j in range(OB):
                d = g * OB + j
                v = psum[d, pl.ds(0, SIZES[q])] + placed(q, d, far)
                outp[g // N, g % N, j, dr(q)] = v.astype(BF16)
            return carry
        lax.fori_loop(0, N * N, body, 0)

    rs1, rs2 = {}, {}

    def src1(q, h, da):
        if h == 0:
            return outp.at[:, (y + da + N) % N, pl.ds(0, HB), dr(q)]
        return outp.at[(x + da + N) % N, :, pl.ds(HB, HB), dr(q)]

    def src2(q, h, db):
        return o2.at[h, ((x if h == 0 else y) + db + N) % N, :, dr(q)]

    def rs_a(q):
        for n, d in enumerate(RING):
            for h in (0, 1):
                rs1[q, h, n] = rcopy(src1(q, h, d), r1.at[h, n, :, :, dr(q)], ring2[h][d])

    def rs_b(q):
        for h in (0, 1):
            total = src1(q, h, 0)[...].astype(F32)
            for n in range(3):
                rs1[q, h, n].wait_recv()
                total = total + r1[h, n, :, :, dr(q)].astype(F32)
            o2[h, :, :, dr(q)] = total.astype(BF16)
            for n, d in enumerate(RING):
                rs2[q, h, n] = rcopy(src2(q, h, d), r2.at[h, n, :, dr(q)], ring1[h][d])

    def rs_c(q):
        for h in (0, 1):
            total = src2(q, h, 0)[...].astype(F32)
            for n in range(3):
                rs2[q, h, n].wait_recv()
                total = total + r2[h, n, :, dr(q)].astype(F32)
            res[pl.ds(h * HB, HB), dr(q)] = total

    inv_in.wait()
    dn_in.wait()
    d_c.wait_recv()
    for q in range(Q):
        for c in d_n[q]:
            c.wait_recv()
        down_dots(q, near)
        if q == 0:
            d_near(1)
        for c in d_fwd[q]:
            c.wait_recv()
        d_far[q] = same(wd.at[slot(2), dr(q)], pr)
        d_near(q + 2)
        place_near(q)
        if q > 0:
            rs_b(q - 1)
        d_far[q].wait_recv()
        down_dots(q, far)
        place_far(q)
        rs_a(q)
        if q > 0:
            rs_c(q - 1)
    rs_b(Q - 1)
    rs_c(Q - 1)

    for j in range(OB):
        out[:, pl.ds(j * BLK, BLK)] = res[j].T
    for c in sent:
        c.wait_send()


def per_device(tokens, up_weight, down_weight, up_index, down_index, up_bias, down_bias):
    smem = pl.BlockSpec(memory_space=pltpu.SMEM)
    vmem = pl.BlockSpec(memory_space=pltpu.VMEM)
    hbm = pl.BlockSpec(memory_space=pl.ANY)
    total = pl.pallas_call(
        kernel,
        out_shape=jax.ShapeDtypeStruct(tokens.shape, F32),
        in_specs=[smem, vmem, hbm, hbm, hbm, vmem],
        out_specs=vmem,
        scratch_shapes=[
            pltpu.VMEM((DB, TOK, BLK), BF16),
            pltpu.VMEM((KB, BLK, CB * BLK), BF16),
            pltpu.VMEM((KB, BLK, CB * BLK), BF16),
            pltpu.VMEM((CB, TOK, BLK), F32),
            pltpu.VMEM((CB, BLK, TOK), BF16),
            pltpu.VMEM((KB, CB + 1, CH, TOK), F32),
            pltpu.VMEM((DB, CH, TOK), F32),
            pltpu.VMEM((N, N, OB, BLK, TOK), BF16),
            pltpu.VMEM((2, 3, N, HB, BLK, TOK), BF16),
            pltpu.VMEM((2, N, HB, BLK, TOK), BF16),
            pltpu.VMEM((2, 3, HB, BLK, TOK), BF16),
            pltpu.VMEM((OB, BLK, TOK), F32),
            pltpu.VMEM((KB, BLK), jnp.int32),
            pltpu.SMEM((KB, BLK), jnp.int32),
            pltpu.SemaphoreType.DMA((NSEM,)),
            pltpu.SemaphoreType.DMA((NSEM,)),
            pltpu.SemaphoreType.DMA((9,)),
        ],
        compiler_params=pltpu.CompilerParams(
            collective_id=0, has_side_effects=True, vmem_limit_bytes=48 * 2**20),
    )(up_index, down_index, tokens, up_weight, down_weight, up_bias.reshape(1, -1))
    return (total + down_bias[None]).astype(BF16)


def solution(mesh):
    placed = (
        P("row", "col"),
        P("row", "col"),
        P("row", "col"),
        P(None, "col"),
        P(None, "col"),
        P("col"),
        P("col"),
    )
    return jax.shard_map(
        per_device, mesh=mesh, in_specs=placed, out_specs=P("row", "col"), check_vma=False
    )
```

```python
import jax
import jax.numpy as jnp
from jax import lax
from jax.experimental import pallas as pl
from jax.experimental.pallas import tpu as pltpu
from jax.sharding import PartitionSpec as P

BLK = 128
KB = 8
N = 4
DB = 96
CB = 24
OB = 6
HB = 3
TOK = 128
SIZES = (32, 32, 32, 16, 16)
STARTS = tuple(sum(SIZES[:q]) for q in range(len(SIZES)))
Q = len(SIZES)
CH = max(SIZES)
NSEM = 180
UP_UNROLL = 4
DN_UNROLL = 8
MESH = pl.DeviceIdType.MESH
F32 = jnp.float32
BF16 = jnp.bfloat16


def kernel(up_idx, dn_idx, tok, up, dn, ub, out,
           feat, wu, wd, acc, ht, prod, psum, outp, r1, o2, r2, res, inv_v, inv,
           ssem, rsem, lsem):
    row = lax.axis_index("row")
    col = lax.axis_index("col")
    z, k = row // 2, row % 2
    x, y = col // N, col % N
    slot = lambda dz: ((z + dz + N) % N) * 2 + k
    zpair = lambda dz: (z + dz + N) % N
    cidx = lambda dx, dy: ((x + dx + N) % N) * N + (y + dy + N) % N
    zp, zm, pr = (slot(1), col), (slot(-1), col), (z * 2 + 1 - k, col)
    xd = {d: (row, cidx(d, 0)) for d in (1, -1, 2)}
    yd = {d: (row, cidx(0, d)) for d in (1, -1, 2)}
    RING = (1, -1, 2)

    local = []

    def lcopy(src, dst):
        c = pltpu.make_async_copy(src, dst, lsem.at[len(local)])
        c.start()
        local.append(c)
        return c

    tok_in = [lcopy(tok.at[:, pl.ds(j * BLK, BLK)], feat.at[col * OB + j]) for j in range(OB)]
    up_in = lcopy(up, wu.at[row])
    dn_in = lcopy(dn, wd.at[row])

    barrier = pltpu.get_barrier_semaphore()
    peers = [zp, zm, pr] + list(xd.values()) + list(yd.values())
    for dev in peers:
        pl.semaphore_signal(barrier, inc=1, device_id=dev, device_id_type=MESH)

    lanes = lax.broadcasted_iota(jnp.int32, (KB, BLK), 1)
    where = jnp.full((KB, BLK), CB, jnp.int32)
    for r in range(CB):
        where = jnp.where(dn_idx[:, r:r + 1] == lanes, r, where)
    inv_v[...] = where
    prod[:, CB] = jnp.zeros((KB, CH, TOK), F32)

    pl.semaphore_wait(barrier, len(peers))

    sent = []

    def rcopy(src, dst, dev):
        i = len(sent)
        c = pltpu.make_async_remote_copy(
            src_ref=src, dst_ref=dst, send_sem=ssem.at[i], recv_sem=rsem.at[i],
            device_id=dev, device_id_type=MESH)
        c.start()
        sent.append(c)
        return c

    def same(ref, dev):
        return rcopy(ref, ref, dev)

    half = BLK // 2
    ur = lambda h: pl.ds(h * half, half)
    u_p = [rcopy(up.at[ur(h)], wu.at[row, ur(h)], zp) for h in (0, 1)]
    u_m = [rcopy(up.at[ur(h)], wu.at[row, ur(h)], zm) for h in (1, 0)]
    u_c = rcopy(up, wu.at[row], pr)

    for c in tok_in:
        c.wait()

    def chunk(h, da):
        dx, dy = (da, 0) if h == 0 else (0, da)
        return pl.ds(cidx(dx, dy) * OB + h * HB, HB)

    ring1, ring2 = (xd, yd), (yd, xd)
    t1 = [[same(feat.at[chunk(h, 0)], ring1[h][d]) for d in RING] for h in (0, 1)]
    t2 = [[], []]

    def spread(h, da):
        t2[h] += [same(feat.at[chunk(h, da)], ring2[h][d]) for d in RING]

    for h in (0, 1):
        spread(h, 0)
    for n, d in enumerate(RING):
        for h in (0, 1):
            t1[h][n].wait_recv()
            spread(h, -d)

    u_p[0].wait_recv()
    u_m[0].wait_recv()
    u_f = [same(wu.at[slot(-1), ur(0)], zp), same(wu.at[slot(1), ur(1)], zm)]

    dr = lambda q: pl.ds(STARTS[q], SIZES[q])
    d_own, d_fwd, d_n, d_far = {}, {}, {}, {}

    def d_issue(q):
        if q < Q:
            d_own[q] = [rcopy(dn.at[dr(q)], wd.at[row, dr(q)], d) for d in (zp, zm)]

    hc = lambda i: pl.ds(i * (CB * BLK // 2), CB * BLK // 2)

    def d_near(q):
        if q < Q:
            for c in d_own[q]:
                c.wait_recv()
            d_fwd[q] = [same(wd.at[slot(-1), dr(q), hc(0)], zp),
                        same(wd.at[slot(1), dr(q), hc(1)], zm)]
            d_issue(q + 2)
            d_n[q] = [same(wd.at[slot(-1), dr(q)], pr), same(wd.at[slot(1), dr(q)], pr)]

    d_issue(0)
    d_issue(1)
    d_c = rcopy(dn, wd.at[row], pr)

    inv_in = lcopy(inv_v, inv)
    u_p[1].wait_recv()
    u_m[1].wait_recv()
    u_n = [same(wu.at[slot(-1)], pr), same(wu.at[slot(1)], pr)]
    for h in (0, 1):
        for c in t2[h]:
            c.wait_recv()
    up_in.wait()
    u_c.wait_recv()
    for c in u_n:
        c.wait_recv()

    def cols(c):
        return pl.ds(pl.multiple_of(c * BLK, BLK), BLK)

    def up_dot(p, c):
        xs = jnp.concatenate([feat[up_idx[2 * p, c]], feat[up_idx[2 * p + 1, c]]], axis=1)
        w = wu[pl.ds(2 * p, 2), :, cols(c)]
        return jnp.dot(xs, w.reshape(2 * BLK, BLK), preferred_element_type=F32)

    def up_first(c, carry):
        acc[c] = up_dot(zpair(0), c) + up_dot(zpair(-1), c) + up_dot(zpair(1), c)
        return carry

    lax.fori_loop(0, CB, up_first, 0, unroll=UP_UNROLL)

    for c in u_f:
        c.wait_recv()
    u_far = same(wu.at[slot(2)], pr)
    u_far.wait_recv()

    def up_last(c, carry):
        v = acc[c] + up_dot(zpair(2), c) + ub[:, cols(c)]
        g = 0.5 * v * (1.0 + jnp.tanh(0.7978845608028654 * (v + 0.044715 * (v * v * v))))
        ht[c] = g.T.astype(BF16)
        return carry

    lax.fori_loop(0, CB // 2, up_last, 0, unroll=UP_UNROLL)
    d_near(0)
    lax.fori_loop(CB // 2, CB, up_last, 0, unroll=UP_UNROLL)

    def down_dots(q, dzs):
        n = SIZES[q]

        def body(r, carry):
            w = jnp.concatenate(
                [wd[pl.ds(2 * zpair(dz), 2), dr(q), cols(r)].reshape(2 * n, BLK) for dz in dzs],
                axis=0)
            o = jnp.dot(w, ht[r], preferred_element_type=F32)
            for i, dz in enumerate(dzs):
                prod[pl.ds(2 * zpair(dz), 2), r, pl.ds(0, n)] = (
                    o[2 * n * i:2 * n * (i + 1)].reshape(2, n, TOK))
            return carry

        lax.fori_loop(0, CB, body, 0, unroll=DN_UNROLL)

    near, far = (0, -1, 1), (2,)

    def placed(q, d, dzs):
        terms = []
        for dz in dzs:
            for i in (0, 1):
                s = 2 * zpair(dz) + i
                terms.append(prod[s, inv[s, d], pl.ds(0, SIZES[q])])
        while len(terms) > 1:
            terms = [a + b for a, b in zip(terms[::2], terms[1::2])] + (
                [terms[-1]] if len(terms) % 2 else [])
        return terms[0]

    def place_near(q):
        def body(g, carry):
            for j in range(OB):
                d = g * OB + j
                psum[d, pl.ds(0, SIZES[q])] = placed(q, d, near)
            return carry
        lax.fori_loop(0, N * N, body, 0)

    def place_far(q):
        def body(g, carry):
            for j in range(OB):
                d = g * OB + j
                v = psum[d, pl.ds(0, SIZES[q])] + placed(q, d, far)
                outp[g // N, g % N, j, dr(q)] = v.astype(BF16)
            return carry
        lax.fori_loop(0, N * N, body, 0)

    def place_all(q):
        def body(g, carry):
            for j in range(OB):
                outp[g // N, g % N, j, dr(q)] = placed(q, g * OB + j, near + far).astype(BF16)
            return carry
        lax.fori_loop(0, N * N, body, 0)

    def far_send(q):
        if q < Q:
            for c in d_fwd[q]:
                c.wait_recv()
            d_far[q] = same(wd.at[slot(2), dr(q)], pr)

    rs1, rs2 = {}, {}

    def src1(q, h, da):
        if h == 0:
            return outp.at[:, (y + da + N) % N, pl.ds(0, HB), dr(q)]
        return outp.at[(x + da + N) % N, :, pl.ds(HB, HB), dr(q)]

    def src2(q, h, db):
        return o2.at[h, ((x if h == 0 else y) + db + N) % N, :, dr(q)]

    def rs_a(q):
        for n, d in enumerate(RING):
            for h in (0, 1):
                rs1[q, h, n] = rcopy(src1(q, h, d), r1.at[h, n, :, :, dr(q)], ring2[h][d])

    def rs_b(q):
        for h in (0, 1):
            total = src1(q, h, 0)[...].astype(F32)
            for n in range(3):
                rs1[q, h, n].wait_recv()
                total = total + r1[h, n, :, :, dr(q)].astype(F32)
            o2[h, :, :, dr(q)] = total.astype(BF16)
            for n, d in enumerate(RING):
                rs2[q, h, n] = rcopy(src2(q, h, d), r2.at[h, n, :, dr(q)], ring1[h][d])

    def rs_c(q):
        for h in (0, 1):
            total = src2(q, h, 0)[...].astype(F32)
            for n in range(3):
                rs2[q, h, n].wait_recv()
                total = total + r2[h, n, :, dr(q)].astype(F32)
            res[pl.ds(h * HB, HB), dr(q)] = total

    inv_in.wait()
    dn_in.wait()
    d_c.wait_recv()
    for q in range(Q):
        for c in d_n[q]:
            c.wait_recv()
        if q == 0:
            down_dots(q, near)
            d_near(1)
            far_send(0)
            d_near(2)
            place_near(q)
            d_far[q].wait_recv()
            down_dots(q, far)
            far_send(1)
            place_far(q)
        else:
            d_far[q].wait_recv()
            down_dots(q, near + far)
            far_send(q + 1)
            d_near(q + 2)
            rs_b(q - 1)
            place_all(q)
        rs_a(q)
        if q > 0:
            rs_c(q - 1)
    rs_b(Q - 1)
    rs_c(Q - 1)

    for j in range(OB):
        out[:, pl.ds(j * BLK, BLK)] = res[j].T
    for c in sent:
        c.wait_send()


def per_device(tokens, up_weight, down_weight, up_index, down_index, up_bias, down_bias):
    smem = pl.BlockSpec(memory_space=pltpu.SMEM)
    vmem = pl.BlockSpec(memory_space=pltpu.VMEM)
    hbm = pl.BlockSpec(memory_space=pl.ANY)
    total = pl.pallas_call(
        kernel,
        out_shape=jax.ShapeDtypeStruct(tokens.shape, F32),
        in_specs=[smem, vmem, hbm, hbm, hbm, vmem],
        out_specs=vmem,
        scratch_shapes=[
            pltpu.VMEM((DB, TOK, BLK), BF16),
            pltpu.VMEM((KB, BLK, CB * BLK), BF16),
            pltpu.VMEM((KB, BLK, CB * BLK), BF16),
            pltpu.VMEM((CB, TOK, BLK), F32),
            pltpu.VMEM((CB, BLK, TOK), BF16),
            pltpu.VMEM((KB, CB + 1, CH, TOK), F32),
            pltpu.VMEM((DB, CH, TOK), F32),
            pltpu.VMEM((N, N, OB, BLK, TOK), BF16),
            pltpu.VMEM((2, 3, N, HB, BLK, TOK), BF16),
            pltpu.VMEM((2, N, HB, BLK, TOK), BF16),
            pltpu.VMEM((2, 3, HB, BLK, TOK), BF16),
            pltpu.VMEM((OB, BLK, TOK), F32),
            pltpu.VMEM((KB, BLK), jnp.int32),
            pltpu.SMEM((KB, BLK), jnp.int32),
            pltpu.SemaphoreType.DMA((NSEM,)),
            pltpu.SemaphoreType.DMA((NSEM,)),
            pltpu.SemaphoreType.DMA((9,)),
        ],
        compiler_params=pltpu.CompilerParams(
            collective_id=0, has_side_effects=True, vmem_limit_bytes=48 * 2**20),
    )(up_index, down_index, tokens, up_weight, down_weight, up_bias.reshape(1, -1))
    return (total + down_bias[None]).astype(BF16)


def solution(mesh):
    placed = (
        P("row", "col"),
        P("row", "col"),
        P("row", "col"),
        P(None, "col"),
        P(None, "col"),
        P("col"),
        P("col"),
    )
    return jax.shard_map(
        per_device, mesh=mesh, in_specs=placed, out_specs=P("row", "col"), check_vma=False
    )
```
